256 devices in a mesh: node: 32 (over y, x, core), local: 8 (over z).
Axes of the slice: x: 4, y: 4, z: 8, core: 2. Of those that a mesh axis runs over, the one named last changes fastest.
Arguments:
- tokens: bfloat16 [2048, 7168], P(('node', 'local')), may hold values from -6 to 6
- grad_out: bfloat16 [2048, 7168], P(('node', 'local')), may hold values from -6 to 6
- expert_ids: int32 [2048, 4], P(('node', 'local')), may hold values from 0 to 31, all different within a row; in each aligned block of 8 rows (0 to 7, 8 to 15, ...) at most 2 rows name the same one
- gate_weights: bfloat16 [2048, 4], P(('node', 'local')), may hold values from 0.049804688 to 1
- w_gate: bfloat16 [32, 7168, 1024], P('node', None, 'local'), may hold values from -0.0625 to 0.0625
- w_up: bfloat16 [32, 7168, 1024], P('node', None, 'local'), may hold values from -0.0625 to 0.0625
- w_down: bfloat16 [32, 1024, 7168], P('node', 'local'), may hold values from -0.1875 to 0.1875
Outputs:
- grad_in: bfloat16 [2048, 7168], P(('node', 'local'))
- grad_gate: bfloat16 [2048, 4], P(('node', 'local'))
- grad_w_gate: bfloat16 [32, 7168, 1024], P('node', None, 'local')
- grad_w_up: bfloat16 [32, 7168, 1024], P('node', None, 'local')
- grad_w_down: bfloat16 [32, 1024, 7168], P('node', 'local')
The draws below stay inside these ranges and needn't reach their ends.
Inputs may be any that keep to these rules, and one draw needn't show every extreme that they name: `expert_ids`: the 4 experts of a token differ. Among one device's 8 tokens no expert is named more than 2 times, and in every draw some expert is named exactly 2 times by some device.
All inputs are finite; a program needn't handle non-finite values.
Results may differ from the reference program's by a relative error of at most 0.024.
Values may be sent and summed in bfloat16 or wider, within the bound.
A program may use at most 128 MiB of HBM per device.

```python
import math
import jax
import jax.numpy as jnp
import numpy as np
from jax import lax

D = 7168
HID = 1024
TOP = 4
TOK_DEV = 8
EXPERTS = 32
HID_DEV = 128
CAP = 2
TOKENS = 2048
N_LOCAL = 8
DEVICES = 256


def level_of(rng, dims, shards, smallest, high):
    gain, own = 1.0, jax.random.fold_in(rng, 6)
    for position, parts in shards:
        draws = jnp.exp(jax.random.uniform(jax.random.fold_in(own, position), (parts,), jnp.float32, smallest / len(shards), high / len(shards)))
        gain = gain * jnp.repeat(draws, dims[position] // parts).reshape([-1 if axis == position else 1 for axis in range(len(dims))])
    return gain


def shared_out(stream_key, own, number, rows, number_of, top, reach, lean):
    order = jax.random.permutation(stream_key, number_of)
    crowded, common = portions_of(number_of, rows * top, reach, lean, True), portions_of(number_of, rows * top, reach, lean, False)
    places = jnp.arange(number_of)

    def named(sizes, rotation):
        used = int((sizes > 0).sum())
        fixed = max(1, used // 4)
        moved = fixed + (places - fixed + rotation * (used - fixed)) % max(1, number_of - fixed)
        return jnp.zeros((number_of,), jnp.int32).at[order[jnp.where(places < fixed, places, moved)]].set(jnp.asarray(sizes, jnp.int32))

    sizes = jnp.where(number % 4 == 0, named(crowded, number // 4), named(common, number - number // 4 - 1))
    mixed = jax.random.permutation(jax.random.fold_in(own, 3), number_of)
    giver, receiver = mixed[0:number_of // 2 * 2:2], mixed[1:number_of // 2 * 2:2]
    slack = jnp.minimum(sizes[giver] - 1, reach - sizes[receiver]) // 2
    slack = jnp.where((giver == order[0]) | (receiver == order[0]) | (sizes[receiver] == 0), 0, jnp.maximum(slack, 0))
    moved = jax.random.randint(jax.random.fold_in(own, 4), (number_of // 2,), 0, 1 << 20) % (slack + 1)
    sizes = sizes.at[giver].add(-moved).at[receiver].add(moved)
    labels = jnp.searchsorted(jnp.cumsum(sizes), jnp.arange(rows * top), side="right").astype(jnp.int32)
    listing = labels.reshape(top, rows).T
    listing = listing[jax.random.permutation(jax.random.fold_in(own, 1), rows)]
    rotation = jax.random.randint(jax.random.fold_in(own, 2), (rows, 1), 0, top)
    return jnp.take_along_axis(listing, (jnp.arange(top)[None, :] + rotation) % top, axis=1)


def portions_of(amount, total, limit, lean, full):
    weights = [(1 << 20) // math.isqrt(grade ** lean) + 1 for grade in range(1, amount + 1)]
    largest = limit if full else min(limit, max(-(-total // amount), total * weights[0] // sum(weights)))
    least = 1 if total - largest >= amount - 1 else 0
    counts, spare = [largest] + [least] * (amount - 1), total - largest - least * (amount - 1)
    while spare > 0:
        free = [i for i in range(1, amount) if counts[i] < largest] or [i for i in range(1, amount) if counts[i] < limit]
        whole, left = sum([weights[i] for i in free]), spare
        for i in free:
            more = min(limit - counts[i], max(1, left * weights[i] // whole), spare)
            counts[i] = counts[i] + more
            spare = spare - more
    return np.array(counts)


def noise(own_key, dims, deviation, reach, shards=(), kind=jnp.bfloat16):
    level = level_of(own_key, dims, shards, -0.22, 0.18) if shards else 1.0
    values = jax.random.normal(own_key, dims, jnp.float32) * deviation * level
    return jnp.minimum(jnp.maximum(values, -reach), reach).astype(kind)


def setup_inputs(seed: int = 0) -> dict:
    streams_of = jax.random.split(jax.random.key(seed), 8)
    tokens = noise(streams_of[0], (TOKENS, D), 1.0, 6.0, ((0, 256),))
    grad_out = noise(streams_of[1], (TOKENS, D), 1.0, 6.0, ((0, 256),))
    expert_ids_keys = jax.random.split(jax.random.fold_in(streams_of[2], 1), TOKENS // TOK_DEV)
    expert_ids_turns = jax.random.permutation(jax.random.fold_in(streams_of[2], 3), TOKENS // TOK_DEV)
    expert_ids = jax.vmap(lambda own, number: shared_out(jax.random.fold_in(streams_of[2], 2), own, number, TOK_DEV, EXPERTS, TOP, CAP, 2))(expert_ids_keys, expert_ids_turns).reshape((TOKENS, TOP))
    gate_weights = jnp.clip(jnp.exp(math.log(1.0) - 2.9996462 * jax.random.uniform(streams_of[3], (TOKENS, TOP), jnp.float32) ** level_of(streams_of[3], (TOKENS, TOP), ((0, 256),), -0.2, 0.2)), 0.049804688, 1.0).astype(jnp.bfloat16)
    w_gate = noise(streams_of[4], (EXPERTS, D, HID), D ** -0.5, 0.0625, ((0, 32), (2, 8)))
    w_up = noise(streams_of[5], (EXPERTS, D, HID), D ** -0.5, 0.0625, ((0, 32), (2, 8)))
    w_down = noise(streams_of[6], (EXPERTS, HID, D), HID ** -0.5, 0.1875, ((0, 32), (1, 8)))
    return {"tokens": tokens, "grad_out": grad_out, "expert_ids": expert_ids, "gate_weights": gate_weights, "w_gate": w_gate, "w_up": w_up, "w_down": w_down}


def silu_parts(gate_pre):
    sigmoid_val = jax.nn.sigmoid(gate_pre)
    return gate_pre * sigmoid_val, sigmoid_val * (1.0 + gate_pre * (1.0 - sigmoid_val))


def reference(tokens, grad_out, expert_ids, gate_weights, w_gate, w_up, w_down):
    onehot = (expert_ids[:, :, None] == jnp.arange(EXPERTS, dtype=jnp.int32)[None, None, :]).astype(jnp.int32)
    per_token = jnp.sum(onehot, axis=1).reshape(DEVICES, TOK_DEV, EXPERTS)
    earlier = (jnp.cumsum(per_token, axis=1) - per_token).reshape(TOKENS, EXPERTS)
    slot_index = jnp.sum(earlier[:, None, :] * onehot, axis=2).astype(jnp.int32)
    device_row = ((jnp.arange(TOKENS, dtype=jnp.int32) // TOK_DEV)[:, None] * CAP + slot_index).astype(jnp.int32)
    token_index = jnp.broadcast_to(jnp.arange(TOKENS, dtype=jnp.int32)[:, None], (TOKENS, TOP))
    choice_index = jnp.broadcast_to(jnp.arange(TOP, dtype=jnp.int32)[None, :], (TOKENS, TOP))
    rows_total = DEVICES * CAP
    table_token = jnp.zeros((EXPERTS, rows_total), jnp.int32).at[expert_ids, device_row].set(token_index)
    table_choice = jnp.zeros((EXPERTS, rows_total), jnp.int32).at[expert_ids, device_row].set(choice_index)
    table_live = jnp.zeros((EXPERTS, rows_total), jnp.int32).at[expert_ids, device_row].set(1)

    def compute_expert(expert):
        rows_token = table_token[expert]
        live = table_live[expert]
        rows_in = tokens[rows_token] * live[:, None].astype(tokens.dtype)
        rows_grad = grad_out[rows_token] * live[:, None].astype(grad_out.dtype)
        rows_gate = gate_weights[rows_token, table_choice[expert]].astype(jnp.float32) * live.astype(jnp.float32)
        gate_proj = w_gate[expert]
        up_proj = w_up[expert]
        down_proj = w_down[expert]
        gate_pre = jnp.dot(rows_in, gate_proj, preferred_element_type=jnp.float32)
        up_pre = jnp.dot(rows_in, up_proj, preferred_element_type=jnp.float32)
        activated, slope = silu_parts(gate_pre)
        hidden = (activated * up_pre).astype(jnp.bfloat16)
        grad_hidden = jnp.dot(rows_grad, down_proj.T, preferred_element_type=jnp.float32)
        shard_sums = jnp.sum((hidden.astype(jnp.float32) * grad_hidden).reshape(rows_total, N_LOCAL, HID_DEV), axis=2)
        shard_sums = lax.optimization_barrier(shard_sums.astype(jnp.bfloat16))
        gate_rows = jnp.sum(shard_sums.astype(jnp.float32), axis=1).astype(jnp.bfloat16)
        scaled = rows_gate[:, None] * grad_hidden
        grad_gate_pre = (scaled * up_pre * slope).astype(jnp.bfloat16)
        grad_up_pre = (scaled * activated).astype(jnp.bfloat16)
        weighted = (rows_gate[:, None] * hidden.astype(jnp.float32)).astype(jnp.bfloat16)
        grad_down = jnp.dot(weighted.T, rows_grad, preferred_element_type=jnp.float32).astype(jnp.bfloat16)
        grad_gate_w = jnp.dot(rows_in.T, grad_gate_pre, preferred_element_type=jnp.float32).astype(jnp.bfloat16)
        grad_up_w = jnp.dot(rows_in.T, grad_up_pre, preferred_element_type=jnp.float32).astype(jnp.bfloat16)
        partial_gate = jnp.einsum("rlh,dlh->lrd", grad_gate_pre.astype(jnp.float32).reshape(rows_total, N_LOCAL, HID_DEV), gate_proj.astype(jnp.float32).reshape(D, N_LOCAL, HID_DEV))
        partial_up = jnp.einsum("rlh,dlh->lrd", grad_up_pre.astype(jnp.float32).reshape(rows_total, N_LOCAL, HID_DEV), up_proj.astype(jnp.float32).reshape(D, N_LOCAL, HID_DEV))
        partial_value = lax.optimization_barrier((partial_gate + partial_up).astype(jnp.bfloat16))
        contrib = jnp.sum(partial_value.astype(jnp.float32), axis=0).astype(jnp.bfloat16)
        return contrib, gate_rows, grad_gate_w, grad_up_w, grad_down

    contrib, gate_rows, grad_w_gate, grad_w_up, grad_w_down = lax.map(compute_expert, jnp.arange(EXPERTS, dtype=jnp.int32))
    flat_token = table_token.reshape(-1)
    flat_choice = table_choice.reshape(-1)
    flat_live = table_live.reshape(-1).astype(jnp.float32)
    grad_in = jnp.zeros((TOKENS, D), jnp.float32).at[flat_token].add(contrib.reshape(-1, D).astype(jnp.float32) * flat_live[:, None]).astype(jnp.bfloat16)
    grad_gate = jnp.zeros((TOKENS, TOP), jnp.float32).at[flat_token, flat_choice].add(gate_rows.reshape(-1).astype(jnp.float32) * flat_live).astype(jnp.bfloat16)
    return grad_in, grad_gate, grad_w_gate, grad_w_up, grad_w_down
```

```python
import jax
import jax.numpy as jnp
from jax import lax
from jax.experimental import pallas as pl
from jax.experimental.pallas import tpu as pltpu
from jax.sharding import PartitionSpec as P

MESH = pl.DeviceIdType.MESH
BF = jnp.bfloat16
F32 = jnp.float32
NODES = 32
NL = 8
TOK = 8
TOP = 4
ROWS = 512
D = 7168
HB = 128
W = 512
DA = D - NL * W
PW = 1024
NP = DA // PW
HALF = ROWS // 2

K_META, K_TB, K_TA, K_GM, K_B, K_A, K_G, K_PA, K_C, K_ZA, K_ZB, K_ZG = 0, 1, 3, 5, 6, 8, 14, 15, 18, 19, 22, 23
K_ALL = 24


def dot(a, b, ca, cb):
    return lax.dot_general(a, b, (((ca,), (cb,)), ((), ())), preferred_element_type=F32)


def aligned(i, m):
    return pl.multiple_of(i, m)


def kernel(tok, gout, meta, wg_h, wu_h, wd_h, gin_o, gg_o, gwg_o, gwu_o, gwd_o,
           wcat, wdv, tgm, tgb, tga, oh, oht, gms, gmr, sb, rb, sa, ra, ab, dh, dadu, hwt,
           pa, backa, gs, gr, rss, rsr, cb, cbr, zas, zar, zbs, zbr, zgs, zgr, gwc, gwd,
           ss, rs, ls, ring_s, ring_r, red_s, red_r, ws, os):
    n = lax.axis_index("node")
    l = lax.axis_index("local")
    cy, cx, cc = lax.div(n, 8), lax.rem(lax.div(n, 2), 4), lax.rem(n, 2)
    right = lax.rem(l + 1, NL)
    left = lax.rem(l + NL - 1, NL)

    weights = [
        pltpu.make_async_copy(wg_h, wcat.at[:, pl.ds(0, HB)], ws.at[0]),
        pltpu.make_async_copy(wu_h, wcat.at[:, pl.ds(HB, HB)], ws.at[1]),
        pltpu.make_async_copy(wd_h, wdv, ws.at[2]),
    ]
    for copy in weights:
        copy.start()

    barrier = pltpu.get_barrier_semaphore()

    def greet_node(i, carry):
        pl.semaphore_signal(barrier, inc=1, device_id=(lax.rem(n + i, NODES), l), device_id_type=MESH)
        return carry

    def greet_local(i, carry):
        pl.semaphore_signal(barrier, inc=1, device_id=(n, lax.rem(l + i, NL)), device_id_type=MESH)
        return carry

    lax.fori_loop(1, NODES, greet_node, 0)
    lax.fori_loop(1, NL, greet_local, 0)
    pl.semaphore_wait(barrier, NODES - 1 + NL - 1)

    def remote(src, dst, ssem, rsem, target):
        return pltpu.make_async_remote_copy(
            src_ref=src, dst_ref=dst, send_sem=ssem, recv_sem=rsem, device_id=target, device_id_type=MESH
        )

    def far_first(t):
        return (2 + t) - lax.div(t, 2) * (2 * t - 1)

    def partner(i):
        k = lax.div(i, 2)
        a, b = far_first(lax.div(k, 4)), far_first(lax.rem(k, 4))
        dy, dx = a + cc * (b - a), b + cc * (a - b)
        dc = 1 - lax.rem(i, 2)
        return (lax.rem(cy + dy, 4) * 4 + lax.rem(cx + dx, 4)) * 2 + lax.rem(cc + dc, 2)

    mine = pl.ds(aligned(n * 16, 16), 16)

    def node_send(src, dst, k):
        def body(i, carry):
            d = partner(i)
            remote(src.at[pl.ds(aligned(d * 16, 16), 16)], dst.at[mine], ss.at[k], rs.at[k], (d, l)).start()
            return carry

        lax.fori_loop(0, NODES - 1, body, 0)
        pltpu.make_async_copy(src.at[mine], dst.at[mine], ls.at[k]).start()

    def node_wait(src, dst, k):
        part = pl.ds(0, 16 * (NODES - 1))
        remote(src.at[part], dst.at[part], ss.at[k], rs.at[k], (n, right)).wait_recv()
        pltpu.make_async_copy(src.at[mine], dst.at[mine], ls.at[k]).wait()

    def node_done(src, dst, k):
        part = pl.ds(0, 16 * (NODES - 1))
        remote(src.at[part], dst.at[part], ss.at[k], rs.at[k], (n, right)).wait_send()

    def local_send(pick, dst, k):
        def body(i, carry):
            step = lax.div(i + 1, 2)
            d = lax.rem(l + 4 + step * (2 * lax.rem(i, 2) - 1), NL)
            remote(pick(d), dst.at[l], ss.at[k], rs.at[k], (n, d)).start()
            return carry

        lax.fori_loop(0, NL - 1, body, 0)
        pltpu.make_async_copy(pick(l), dst.at[l], ls.at[k]).start()

    def local_wait(pick, dst, k):
        part = pl.ds(0, NL - 1)
        remote(dst.at[part], dst.at[part], ss.at[k], rs.at[k], (n, right)).wait_recv()
        pltpu.make_async_copy(pick(l), dst.at[l], ls.at[k]).wait()

    def local_done(dst, k):
        part = pl.ds(0, NL - 1)
        remote(dst.at[part], dst.at[part], ss.at[k], rs.at[k], (n, right)).wait_send()

    pick_meta = lambda d: meta
    srcs = (tok, gout)
    pick_b = [lambda d, s=s: s.at[:, pl.ds(aligned(DA + d * W, W), W)] for s in srcs]
    pick_a = [lambda d, s=s: s.at[:, pl.ds(0, DA)] for s in srcs]
    local_send(pick_meta, tgm, K_META)
    for t in range(2):
        local_send(pick_b[t], tgb.at[t], K_TB + t)
    for t in range(2):
        local_send(pick_a[t], tga.at[t], K_TA + t)

    local_wait(pick_meta, tgm, K_META)
    info = jnp.sum(tgm[...], axis=0)
    slot = lax.broadcasted_iota(jnp.int32, (ROWS, 128), 0)
    lane = lax.broadcasted_iota(jnp.int32, (ROWS, 128), 1)
    key = (lax.shift_right_logical(slot, 4) * 2 + jnp.bitwise_and(slot, 1) + 1).astype(F32)
    same = lax.shift_right_logical(jnp.bitwise_and(slot, 15), 1) == lax.shift_right_logical(lane, 3)
    key = jnp.where(same, key, -1.0)
    placing = jnp.zeros((ROWS, 128), F32)
    about = jnp.zeros((ROWS, 128), F32)
    for k in range(TOP):
        hit = jnp.where(key == info[k:k + 1, :], 1.0, 0.0)
        placing = placing + hit
        live = jnp.sum(hit, axis=1, keepdims=True)
        gate = jnp.sum(hit * info[TOP + k:TOP + k + 1, :], axis=1, keepdims=True)
        about = about + jnp.where(lane == k, live, 0.0) + jnp.where(lane == TOP + k, gate, 0.0)
    oh[...] = placing[:, :64].astype(BF)
    oht[...] = placing.T[:64, :].astype(BF)
    gms[...] = about.astype(BF)

    def packed(piece):
        rows = piece.astype(F32).reshape(NL * TOK, piece.shape[2]).astype(BF)
        return dot(oh[...], rows, 1, 0).astype(BF)

    for t in range(2):
        local_wait(pick_b[t], tgb.at[t], K_TB + t)
        sb[t] = packed(tgb[t])
        node_send(sb.at[t], rb.at[t, l], K_B + t)
    node_send(gms, gmr, K_GM)

    def send_a(t):
        local_wait(pick_a[t], tga.at[t], K_TA + t)
        for p in range(NP):
            for j in range(PW // W):
                sa[t, p, :, pl.ds(j * W, W)] = packed(tga[t, :, :, pl.ds(p * PW + j * W, W)])
            node_send(sa.at[t, p], ra.at[t, p], K_A + t * NP + p)

    def ring(t, s, d, h):
        c = lax.rem(l - s + NL, NL) if d == 0 else lax.rem(l + s, NL)
        view = rb.at[t, c, pl.ds(h * HALF, HALF)]
        return remote(view, view, ring_s.at[t, s, d, h], ring_r.at[t, s, d, h], (n, right if d == 0 else left))

    def ring_step(t, s):
        for h in range(2):
            for d in range(2):
                if s > 0:
                    ring(t, s - 1, d, h).wait_recv()
                if s < 3 or h == d:
                    ring(t, s, d, h).start()

    def use_b(t, c):
        off = aligned(DA + c * W, W)
        if t == 0:
            ab[...] += dot(rb[0, c], wcat[pl.ds(off, W), :], 1, 0)
        else:
            dh[...] += dot(rb[1, c], wdv[:, pl.ds(off, W)], 1, 1)

    def use_a(t, p):
        node_wait(sa.at[t, p], ra.at[t, p], K_A + t * NP + p)

        def body(j, carry):
            o = aligned(j * W, W)
            off = aligned(p * PW + j * W, W)
            if t == 0:
                ab[...] += dot(ra[0, p, :, pl.ds(o, W)], wcat[pl.ds(off, W), :], 1, 0)
            else:
                dh[...] += dot(ra[1, p, :, pl.ds(o, W)], wdv[:, pl.ds(off, W)], 1, 1)
            return carry

        lax.fori_loop(0, PW // W, body, 0)

    def use_pair(s):
        def body(i, carry):
            c = lax.rem(l + NL - s + 2 * s * i, NL)
            use_b(0, c)
            use_b(1, c)
            return carry

        lax.fori_loop(0, 2, body, 0)

    send_a(0)
    node_wait(sb.at[0], rb.at[0, l], K_B)
    ring_step(0, 0)
    send_a(1)
    node_wait(sb.at[1], rb.at[1, l], K_B + 1)
    ring_step(1, 0)
    for copy in weights:
        copy.wait()
    ab[...] = jnp.zeros_like(ab)
    dh[...] = jnp.zeros_like(dh)
    use_b(0, l)
    use_b(1, l)
    after = {1: ((0, 0), (0, 1)), 2: ((0, 2), (1, 0)), 3: ((1, 1),)}
    for s in (1, 2, 3):
        ring_step(0, s)
        ring_step(1, s)
        use_pair(s)
        for t, p in after[s]:
            use_a(t, p)
    use_a(1, 2)
    opposite = lax.rem(l + 4, NL)
    for t in range(2):
        for d in range(2):
            ring(t, 3, d, d).wait_recv()
        use_b(t, opposite)

    node_wait(gms, gmr, K_GM)
    facts = gmr[...].astype(F32)
    a, b, dhv = ab[:, :HB], ab[:, HB:], dh[...]
    sig = jax.nn.sigmoid(a)
    act = a * sig
    hidden = (act * b).astype(BF).astype(F32)
    total = jnp.sum(hidden * dhv, axis=1, keepdims=True).astype(BF).astype(F32)
    gs[...] = jnp.where(lane < TOP, facts * total, 0.0).astype(BF)
    gate = jnp.sum(jnp.where((lane >= TOP) & (lane < 2 * TOP), facts, 0.0), axis=1, keepdims=True)
    scaled = gate * dhv
    dadu[:, :HB] = (scaled * b * (sig * (1.0 + a * (1.0 - sig)))).astype(BF)
    dadu[:, HB:] = (scaled * act).astype(BF)
    hwt[...] = (gate * hidden).T.astype(BF)

    def partial(c, h):
        return dot(dadu[h * HALF:(h + 1) * HALF, :], wcat[pl.ds(aligned(DA + c * W, W), W), :], 1, 1)

    def reduce_copy(s, d, h):
        return remote(rss.at[s, d, h], rsr.at[s, d, h], red_s.at[s, d, h], red_r.at[s, d, h],
                      (n, right if d == 0 else left))

    def reduce_send(s, d, h):
        c = lax.rem(l + 4 - s, NL) if d == 0 else lax.rem(l + 4 + s, NL)
        term = partial(c, h)
        if s > 1 or (s == 1 and h == d):
            reduce_copy(s - 1, d, h).wait_recv()
            term = term + rsr[s - 1, d, h].astype(F32)
        rss[s, d, h] = term.astype(BF)
        reduce_copy(s, d, h).start()

    def send_pa(p):
        def body(j, carry):
            o = aligned(j * W, W)
            pa[p, :, pl.ds(o, W)] = dot(dadu[...], wcat[pl.ds(aligned(p * PW + j * W, W), W), :], 1, 1).astype(BF)
            return carry

        lax.fori_loop(0, PW // W, body, 0)
        node_send(pa.at[p], backa.at[p], K_PA + p)

    def weight_grads(x, dy, off):
        gwc[pl.ds(off, W), :] = dot(x, dadu[...], 0, 0).astype(BF)
        gwd[:, pl.ds(off, W)] = dot(hwt[...], dy, 1, 0).astype(BF)

    def grads_b(lo, hi):
        def body(c, carry):
            weight_grads(rb[0, c], rb[1, c], aligned(DA + c * W, W))
            return carry

        lax.fori_loop(lo, hi, body, 0)

    def grads_a(p):
        def body(j, carry):
            o = aligned(j * W, W)
            weight_grads(ra[0, p, :, pl.ds(o, W)], ra[1, p, :, pl.ds(o, W)], aligned(p * PW + j * W, W))
            return carry

        lax.fori_loop(0, PW // W, body, 0)

    for d in range(2):
        reduce_send(0, d, d)
    send_pa(0)
    for d in range(2):
        reduce_send(1, d, 1 - d)
    node_send(gs, gr, K_G)
    send_pa(1)
    send_pa(2)
    for d in range(2):
        reduce_send(1, d, d)
    grads_b(0, 3)
    for d in range(2):
        reduce_send(2, d, 1 - d)
    grads_b(3, 6)
    for d in range(2):
        reduce_send(2, d, d)
    grads_b(6, 8)
    for d in range(2):
        reduce_send(3, d, 1 - d)
    grads_a(0)
    for d in range(2):
        reduce_send(3, d, d)
    grads_a(1)
    for h in (1, 0):
        term = partial(l, h)
        for d in range(2):
            reduce_copy(3, d, h).wait_recv()
            term = term + rsr[3, d, h].astype(F32)
        cb[h * HALF:(h + 1) * HALF, :] = term.astype(BF)
    node_send(cb, cbr, K_C)

    def unpack(block):
        rows = dot(oht[...], block, 1, 0)
        return rows.reshape(NL, TOK, block.shape[1]).astype(BF)

    pick_za = [lambda d, p=p: zas.at[p, d] for p in range(NP)]
    for p in range(NP):
        node_wait(pa.at[p], backa.at[p], K_PA + p)
        for j in range(PW // W):
            zas[p, :, :, pl.ds(j * W, W)] = unpack(backa[p, :, pl.ds(j * W, W)])
        local_send(pick_za[p], zar.at[p], K_ZA + p)
    node_wait(gs, gr, K_G)
    pick_zg = lambda d: zgs.at[d]
    zgs[...] = unpack(gr[...])
    local_send(pick_zg, zgr, K_ZG)
    grads_a(2)
    outs = [
        pltpu.make_async_copy(gwc.at[:, pl.ds(0, HB)], gwg_o, os.at[0]),
        pltpu.make_async_copy(gwc.at[:, pl.ds(HB, HB)], gwu_o, os.at[1]),
        pltpu.make_async_copy(gwd, gwd_o, os.at[2]),
    ]
    for copy in outs:
        copy.start()
    pick_zb = lambda d: zbs.at[d]
    node_wait(cb, cbr, K_C)
    zbs[...] = unpack(cbr[...])
    local_send(pick_zb, zbr, K_ZB)

    for p in range(NP):
        local_wait(pick_za[p], zar.at[p], K_ZA + p)
        gin_o[:, p * PW:(p + 1) * PW] = jnp.sum(zar[p].astype(F32), axis=0).astype(BF)
    local_wait(pick_zg, zgr, K_ZG)
    gg_o[...] = jnp.sum(zgr[...].astype(F32), axis=0)
    local_wait(pick_zb, zbr, K_ZB)
    for c in range(NL):
        gin_o[:, DA + c * W:DA + (c + 1) * W] = zbr[c]

    local_done(tgm, K_META)
    node_done(gms, gmr, K_GM)
    node_done(gs, gr, K_G)
    node_done(cb, cbr, K_C)
    local_done(zgr, K_ZG)
    local_done(zbr, K_ZB)
    for t in range(2):
        local_done(tgb.at[t], K_TB + t)
        local_done(tga.at[t], K_TA + t)
        node_done(sb.at[t], rb.at[t, l], K_B + t)
        for p in range(NP):
            node_done(sa.at[t, p], ra.at[t, p], K_A + t * NP + p)
        for s in range(4):
            for d in range(2):
                for h in range(2):
                    if s < 3 or h == d:
                        ring(t, s, d, h).wait_send()
    for p in range(NP):
        node_done(pa.at[p], backa.at[p], K_PA + p)
        local_done(zar.at[p], K_ZA + p)
    for s in range(4):
        for d in range(2):
            for h in range(2):
                if s > 0 or h == d:
                    reduce_copy(s, d, h).wait_send()
    for copy in outs:
        copy.wait()


def per_device(tokens, grad_out, expert_ids, gate_weights, w_gate, w_up, w_down):
    l = lax.axis_index("local")
    named = expert_ids[:, :, None, None] == expert_ids[None, None, :, :]
    before = jnp.arange(TOK)[:, None, None, None] > jnp.arange(TOK)[None, None, :, None]
    slot = jnp.sum((named & before).astype(jnp.int32), axis=(2, 3))
    label = (expert_ids * 2 + slot + 1).astype(F32)
    both = jnp.concatenate([label.T, gate_weights.astype(F32).T], axis=0)
    here = (jnp.arange(128) // TOK == l)[None, :]
    meta = jnp.where(here, jnp.tile(both, (1, 128 // TOK)), 0.0)
    vm = pl.BlockSpec(memory_space=pltpu.VMEM)
    anywhere = pl.BlockSpec(memory_space=pl.ANY)
    shape = jax.ShapeDtypeStruct
    dma = pltpu.SemaphoreType.DMA
    gin, gg, gwg, gwu, gwd = pl.pallas_call(
        kernel,
        out_shape=(
            shape((TOK, D), BF), shape((TOK, 128), F32),
            shape((D, HB), BF), shape((D, HB), BF), shape((HB, D), BF),
        ),
        in_specs=[vm, vm, vm, anywhere, anywhere, anywhere],
        out_specs=(vm, vm, anywhere, anywhere, anywhere),
        scratch_shapes=[
            pltpu.VMEM((D, 2 * HB), BF),
            pltpu.VMEM((HB, D), BF),
            pltpu.VMEM((NL, 8, 128), F32),
            pltpu.VMEM((2, NL, TOK, W), BF),
            pltpu.VMEM((2, NL, TOK, DA), BF),
            pltpu.VMEM((ROWS, NL * TOK), BF),
            pltpu.VMEM((NL * TOK, ROWS), BF),
            pltpu.VMEM((ROWS, 128), BF),
            pltpu.VMEM((ROWS, 128), BF),
            pltpu.VMEM((2, ROWS, W), BF),
            pltpu.VMEM((2, NL, ROWS, W), BF),
            pltpu.VMEM((2, NP, ROWS, PW), BF),
            pltpu.VMEM((2, NP, ROWS, PW), BF),
            pltpu.VMEM((ROWS, 2 * HB), F32),
            pltpu.VMEM((ROWS, HB), F32),
            pltpu.VMEM((ROWS, 2 * HB), BF),
            pltpu.VMEM((HB, ROWS), BF),
            pltpu.VMEM((NP, ROWS, PW), BF),
            pltpu.VMEM((NP, ROWS, PW), BF),
            pltpu.VMEM((ROWS, 128), BF),
            pltpu.VMEM((ROWS, 128), BF),
            pltpu.VMEM((4, 2, 2, HALF, W), BF),
            pltpu.VMEM((4, 2, 2, HALF, W), BF),
            pltpu.VMEM((ROWS, W), BF),
            pltpu.VMEM((ROWS, W), BF),
            pltpu.VMEM((NP, NL, TOK, PW), BF),
            pltpu.VMEM((NP, NL, TOK, PW), BF),
            pltpu.VMEM((NL, TOK, W), BF),
            pltpu.VMEM((NL, TOK, W), BF),
            pltpu.VMEM((NL, TOK, 128), BF),
            pltpu.VMEM((NL, TOK, 128), BF),
            pltpu.VMEM((D, 2 * HB), BF),
            pltpu.VMEM((HB, D), BF),
            dma((K_ALL,)), dma((K_ALL,)), dma((K_ALL,)),
            dma((2, 4, 2, 2)), dma((2, 4, 2, 2)), dma((4, 2, 2)), dma((4, 2, 2)),
            dma((3,)), dma((3,)),
        ],
        compiler_params=pltpu.CompilerParams(
            collective_id=0, has_side_effects=True, vmem_limit_bytes=62 * 2**20
        ),
        name="expert_backward",
    )(tokens, grad_out, meta, w_gate[0], w_up[0], w_down[0])
    return gin, gg[:, :TOP].astype(BF), gwg[None], gwu[None], gwd[None]


def solution(mesh):
    rows = P(("node", "local"), None)
    columns = P("node", None, "local")
    return jax.shard_map(
        per_device,
        mesh=mesh,
        in_specs=(rows, rows, rows, rows, columns, columns, P("node", "local", None)),
        out_specs=(rows, rows, columns, columns, P("node", "local", None)),
        check_vma=False,
    )
```

```python
import jax
import jax.numpy as jnp
from jax import lax
from jax.experimental import pallas as pl
from jax.experimental.pallas import tpu as pltpu
from jax.sharding import PartitionSpec as P

MESH = pl.DeviceIdType.MESH
BF = jnp.bfloat16
F32 = jnp.float32
NODES = 32
NL = 8
TOK = 8
TOP = 4
ROWS = 512
D = 7168
HB = 128
W = 512
DA = D - NL * W
PW = 1024
NP = DA // PW
HALF = ROWS // 2
WH = W // 2

K_META, K_TB, K_TA, K_GM, K_B, K_A, K_G, K_PA, K_C, K_ZA, K_ZB, K_ZG = 0, 1, 3, 5, 6, 10, 16, 17, 20, 21, 24, 25
K_ALL = 26


def dot(a, b, ca, cb):
    return lax.dot_general(a, b, (((ca,), (cb,)), ((), ())), preferred_element_type=F32)


def aligned(i, m):
    return pl.multiple_of(i, m)


def kernel(tok, gout, ids, gates, wg_h, wu_h, wd_h, gin_o, gg_o, gwg_o, gwu_o, gwd_o,
           wcat, wdv, named, meta, tgm, tgb, tga, oh, oht, gms, gmr, sb, rb, sa, ra, ab, dh, dadu, hwt,
           pa, backa, gs, gr, rss, rsr, cb, cbr, zas, zar, zbs, zbr, zgs, zgr,
           ss, rs, ls, ring_s, ring_r, red_s, red_r, tok_s, tok_r, ws):
    n = lax.axis_index("node")
    l = lax.axis_index("local")
    cy, cx, cc = lax.div(n, 8), lax.rem(lax.div(n, 2), 4), lax.rem(n, 2)
    right = lax.rem(l + 1, NL)
    left = lax.rem(l + NL - 1, NL)

    weights = [
        pltpu.make_async_copy(wg_h, wcat.at[:, pl.ds(0, HB)], ws.at[0]),
        pltpu.make_async_copy(wu_h, wcat.at[:, pl.ds(HB, HB)], ws.at[1]),
        pltpu.make_async_copy(wd_h, wdv, ws.at[2]),
    ]
    for copy in weights:
        copy.start()

    barrier = pltpu.get_barrier_semaphore()

    def greet_node(i, carry):
        pl.semaphore_signal(barrier, inc=1, device_id=(lax.rem(n + i, NODES), l), device_id_type=MESH)
        return carry

    def greet_local(i, carry):
        pl.semaphore_signal(barrier, inc=1, device_id=(n, lax.rem(l + i, NL)), device_id_type=MESH)
        return carry

    lax.fori_loop(1, NODES, greet_node, 0)
    lax.fori_loop(1, NL, greet_local, 0)

    named[...] = jnp.full((8, 128), -1.0, F32)
    named[0:TOP, 0:TOK] = ids[...].astype(F32)
    own = named[...]
    count = jnp.zeros((8, 128), F32)
    for k in range(TOP):
        row = jnp.broadcast_to(own[k:k + 1, :], (8, 128))
        for step in range(1, TOK):
            count = count + jnp.where(own == pltpu.roll(row, step, 1), 1.0, 0.0)
    named[...] = 2.0 * own + count + 1.0
    named[TOP:2 * TOP, 0:TOK] = gates[...].astype(F32)
    tokens_lanes = lax.broadcasted_iota(jnp.int32, (8, 128), 1) < TOK
    meta[...] = pltpu.roll(jnp.where(tokens_lanes, named[...], 0.0), l * TOK, 1)
    pl.semaphore_wait(barrier, NODES - 1 + NL - 1)

    def remote(src, dst, ssem, rsem, target):
        return pltpu.make_async_remote_copy(
            src_ref=src, dst_ref=dst, send_sem=ssem, recv_sem=rsem, device_id=target, device_id_type=MESH
        )

    def far_first(t):
        return (2 + t) - lax.div(t, 2) * (2 * t - 1)

    def partner(i):
        k = lax.div(i, 2)
        a, b = far_first(lax.div(k, 4)), far_first(lax.rem(k, 4))
        dy, dx = a + cc * (b - a), b + cc * (a - b)
        dc = 1 - lax.rem(i, 2)
        return (lax.rem(cy + dy, 4) * 4 + lax.rem(cx + dx, 4)) * 2 + lax.rem(cc + dc, 2)

    mine = pl.ds(aligned(n * 16, 16), 16)

    def node_send(src, dst, k):
        def body(i, carry):
            d = partner(i)
            remote(src.at[pl.ds(aligned(d * 16, 16), 16)], dst.at[mine], ss.at[k], rs.at[k], (d, l)).start()
            return carry

        lax.fori_loop(0, NODES - 1, body, 0)
        pltpu.make_async_copy(src.at[mine], dst.at[mine], ls.at[k]).start()

    def node_wait(src, dst, k):
        part = pl.ds(0, 16 * (NODES - 1))
        remote(src.at[part], dst.at[part], ss.at[k], rs.at[k], (n, right)).wait_recv()
        pltpu.make_async_copy(src.at[mine], dst.at[mine], ls.at[k]).wait()

    def node_done(src, dst, k):
        part = pl.ds(0, 16 * (NODES - 1))
        remote(src.at[part], dst.at[part], ss.at[k], rs.at[k], (n, right)).wait_send()

    def local_send(pick, dst, k):
        def body(i, carry):
            step = lax.div(i + 1, 2)
            d = lax.rem(l + 4 + step * (2 * lax.rem(i, 2) - 1), NL)
            remote(pick(d), dst.at[l], ss.at[k], rs.at[k], (n, d)).start()
            return carry

        lax.fori_loop(0, NL - 1, body, 0)
        pltpu.make_async_copy(pick(l), dst.at[l], ls.at[k]).start()

    def local_wait(pick, dst, k):
        part = pl.ds(0, NL - 1)
        remote(dst.at[part], dst.at[part], ss.at[k], rs.at[k], (n, right)).wait_recv()
        pltpu.make_async_copy(pick(l), dst.at[l], ls.at[k]).wait()

    def local_done(dst, k):
        part = pl.ds(0, NL - 1)
        remote(dst.at[part], dst.at[part], ss.at[k], rs.at[k], (n, right)).wait_send()

    pick_meta = lambda d: meta
    srcs = (tok, gout)
    pick_b = [lambda d, s=s: s.at[:, pl.ds(aligned(DA + d * W, W), W)] for s in srcs]
    pick_a = [lambda d, s=s: s.at[:, pl.ds(0, DA)] for s in srcs]
    local_send(pick_meta, tgm, K_META)
    for t in range(2):
        local_send(pick_b[t], tgb.at[t], K_TB + t)

    def tok_ring(t, s, d):
        c = lax.rem(l - s + NL, NL) if d == 0 else lax.rem(l + s, NL)
        dst = tga.at[t, c]
        src = pick_a[t](c) if s == 0 else dst
        return remote(src, dst, tok_s.at[t, s, d], tok_r.at[t, s, d], (n, right if d == 0 else left))

    def tok_step(s):
        for t in range(2):
            for d in range(2):
                if s > 0:
                    tok_ring(t, s - 1, d).wait_recv()
                if s < 3 or d == t:
                    tok_ring(t, s, d).start()

    tok_step(0)
    for t in range(2):
        pltpu.make_async_copy(pick_a[t](l), tga.at[t, l], ls.at[K_TA + t]).start()
    tok_step(1)

    local_wait(pick_meta, tgm, K_META)
    info = jnp.sum(tgm[...], axis=0)
    slot = lax.broadcasted_iota(jnp.int32, (ROWS, 128), 0)
    lane = lax.broadcasted_iota(jnp.int32, (ROWS, 128), 1)
    key = (lax.shift_right_logical(slot, 4) * 2 + jnp.bitwise_and(slot, 1) + 1).astype(F32)
    same = lax.shift_right_logical(jnp.bitwise_and(slot, 15), 1) == lax.shift_right_logical(lane, 3)
    key = jnp.where(same, key, -1.0)
    placing = jnp.zeros((ROWS, 128), F32)
    for k in range(TOP):
        placing = placing + jnp.where(key == info[k:k + 1, :], 1.0, 0.0)
    oh[...] = placing[:, :64].astype(BF)

    def packed(piece):
        rows = piece.astype(F32).reshape(NL * TOK, piece.shape[2]).astype(BF)
        return dot(oh[...], rows, 1, 0).astype(BF)

    for t in range(2):
        local_wait(pick_b[t], tgb.at[t], K_TB + t)
        both = packed(tgb[t])
        for h in range(2):
            sb[t, h] = both[:, h * WH:(h + 1) * WH]
            node_send(sb.at[t, h], rb.at[t, l, h], K_B + 2 * t + h)
        tok_step(2 + t)
    oht[...] = placing.T[:64, :].astype(BF)
    about = jnp.zeros((ROWS, 128), F32)
    for k in range(TOP):
        hit = jnp.where(key == info[k:k + 1, :], 1.0, 0.0)
        live = jnp.sum(hit, axis=1, keepdims=True)
        gate = jnp.sum(hit * info[TOP + k:TOP + k + 1, :], axis=1, keepdims=True)
        about = about + jnp.where(lane == k, live, 0.0) + jnp.where(lane == TOP + k, gate, 0.0)
    gms[...] = about.astype(BF)
    node_send(gms, gmr, K_GM)

    def send_a(t):
        tok_ring(t, 3, t).wait_recv()
        pltpu.make_async_copy(pick_a[t](l), tga.at[t, l], ls.at[K_TA + t]).wait()
        for p in range(NP):
            for j in range(PW // W):
                sa[t, p, :, pl.ds(j * W, W)] = packed(tga[t, :, :, pl.ds(p * PW + j * W, W)])
            node_send(sa.at[t, p], ra.at[t, p], K_A + t * NP + p)

    def ring(t, s, d, h):
        c = lax.rem(l - s + NL, NL) if d == 0 else lax.rem(l + s, NL)
        view = rb.at[t, c, h]
        return remote(view, view, ring_s.at[t, s, d, h], ring_r.at[t, s, d, h], (n, right if d == 0 else left))

    def ring_step(t, s):
        for h in range(2):
            for d in range(2):
                if s == 0 and d == 0:
                    node_wait(sb.at[t, h], rb.at[t, l, h], K_B + 2 * t + h)
                if s > 0:
                    ring(t, s - 1, d, h).wait_recv()
                if s < 3 or h == d:
                    ring(t, s, d, h).start()

    def use_b(t, c):
        for h in range(2):
            off = aligned(DA + c * W + h * WH, WH)
            if t == 0:
                ab[...] += dot(rb[0, c, h], wcat[pl.ds(off, WH), :], 1, 0)
            else:
                dh[...] += dot(rb[1, c, h], wdv[:, pl.ds(off, WH)], 1, 1)

    def use_a(t, p):
        node_wait(sa.at[t, p], ra.at[t, p], K_A + t * NP + p)

        def body(j, carry):
            o = aligned(j * W, W)
            off = aligned(p * PW + j * W, W)
            if t == 0:
                ab[...] += dot(ra[0, p, :, pl.ds(o, W)], wcat[pl.ds(off, W), :], 1, 0)
            else:
                dh[...] += dot(ra[1, p, :, pl.ds(o, W)], wdv[:, pl.ds(off, W)], 1, 1)
            return carry

        lax.fori_loop(0, PW // W, body, 0)

    def use_pair(s):
        def body(i, carry):
            c = lax.rem(l + NL - s + 2 * s * i, NL)
            use_b(0, c)
            use_b(1, c)
            return carry

        lax.fori_loop(0, 2, body, 0)

    send_a(0)
    ring_step(0, 0)
    send_a(1)
    ring_step(1, 0)
    for copy in weights:
        copy.wait()
    ab[...] = jnp.zeros_like(ab)
    dh[...] = jnp.zeros_like(dh)
    use_b(0, l)
    use_b(1, l)
    after = {1: ((0, 0), (0, 1)), 2: ((0, 2), (1, 0)), 3: ((1, 1),)}
    for s in (1, 2, 3):
        ring_step(0, s)
        ring_step(1, s)
        use_pair(s)
        for t, p in after[s]:
            use_a(t, p)
    use_a(1, 2)
    opposite = lax.rem(l + 4, NL)
    for t in range(2):
        for d in range(2):
            ring(t, 3, d, d).wait_recv()
        use_b(t, opposite)

    node_wait(gms, gmr, K_GM)
    facts = gmr[...].astype(F32)
    a, b, dhv = ab[:, :HB], ab[:, HB:], dh[...]
    sig = jax.nn.sigmoid(a)
    act = a * sig
    hidden = (act * b).astype(BF).astype(F32)
    total = jnp.sum(hidden * dhv, axis=1, keepdims=True).astype(BF).astype(F32)
    gs[...] = jnp.where(lane < TOP, facts * total, 0.0).astype(BF)
    gate = jnp.sum(jnp.where((lane >= TOP) & (lane < 2 * TOP), facts, 0.0), axis=1, keepdims=True)
    scaled = gate * dhv
    dadu[:, :HB] = (scaled * b * (sig * (1.0 + a * (1.0 - sig)))).astype(BF)
    dadu[:, HB:] = (scaled * act).astype(BF)
    hwt[...] = (gate * hidden).T.astype(BF)

    def partial(c, h):
        return dot(dadu[h * HALF:(h + 1) * HALF, :], wcat[pl.ds(aligned(DA + c * W, W), W), :], 1, 1)

    def reduce_copy(s, d, h):
        return remote(rss.at[s, d, h], rsr.at[s, d, h], red_s.at[s, d, h], red_r.at[s, d, h],
                      (n, right if d == 0 else left))

    def reduce_send(s, d, h):
        c = lax.rem(l + 4 - s, NL) if d == 0 else lax.rem(l + 4 + s, NL)
        term = partial(c, h)
        if s > 1 or (s == 1 and h == d):
            reduce_copy(s - 1, d, h).wait_recv()
            term = term + rsr[s - 1, d, h].astype(F32)
        rss[s, d, h] = term.astype(BF)
        reduce_copy(s, d, h).start()

    def send_pa(p):
        def body(j, carry):
            o = aligned(j * W, W)
            pa[p, :, pl.ds(o, W)] = dot(dadu[...], wcat[pl.ds(aligned(p * PW + j * W, W), W), :], 1, 1).astype(BF)
            return carry

        lax.fori_loop(0, PW // W, body, 0)
        node_send(pa.at[p], backa.at[p], K_PA + p)

    def weight_grads(x, dy, off, width):
        both = dot(x, dadu[...], 0, 0).astype(BF)
        gwg_o[pl.ds(off, width), :] = both[:, :HB]
        gwu_o[pl.ds(off, width), :] = both[:, HB:]
        gwd_o[:, pl.ds(off, width)] = dot(hwt[...], dy, 1, 0).astype(BF)

    def grads_b(lo, hi):
        def body(c, carry):
            for h in range(2):
                weight_grads(rb[0, c, h], rb[1, c, h], aligned(DA + c * W + h * WH, WH), WH)
            return carry

        lax.fori_loop(lo, hi, body, 0)

    def grads_a(p):
        def body(j, carry):
            o = aligned(j * W, W)
            weight_grads(ra[0, p, :, pl.ds(o, W)], ra[1, p, :, pl.ds(o, W)], aligned(p * PW + j * W, W), W)
            return carry

        lax.fori_loop(0, PW // W, body, 0)

    for d in range(2):
        reduce_send(0, d, d)
    send_pa(0)
    for d in range(2):
        reduce_send(1, d, 1 - d)
    node_send(gs, gr, K_G)
    send_pa(1)
    send_pa(2)
    for d in range(2):
        reduce_send(1, d, d)
    grads_b(0, 3)
    for d in range(2):
        reduce_send(2, d, 1 - d)
    grads_b(3, 6)
    for d in range(2):
        reduce_send(2, d, d)
    grads_b(6, 8)
    for d in range(2):
        reduce_send(3, d, 1 - d)
    grads_a(0)
    for d in range(2):
        reduce_send(3, d, d)
    grads_a(1)
    for h in (1, 0):
        term = partial(l, h)
        for d in range(2):
            reduce_copy(3, d, h).wait_recv()
            term = term + rsr[3, d, h].astype(F32)
        cb[h * HALF:(h + 1) * HALF, :] = term.astype(BF)
    node_send(cb, cbr, K_C)

    def unpack(block):
        rows = dot(oht[...], block, 1, 0)
        return rows.reshape(NL, TOK, block.shape[1]).astype(BF)

    pick_za = [lambda d, p=p: zas.at[p, d] for p in range(NP)]
    for p in range(NP):
        node_wait(pa.at[p], backa.at[p], K_PA + p)
        for j in range(PW // W):
            zas[p, :, :, pl.ds(j * W, W)] = unpack(backa[p, :, pl.ds(j * W, W)])
        local_send(pick_za[p], zar.at[p], K_ZA + p)
    node_wait(gs, gr, K_G)
    pick_zg = lambda d: zgs.at[d]
    zgs[...] = unpack(gr[...])
    local_send(pick_zg, zgr, K_ZG)
    grads_a(2)
    pick_zb = lambda d: zbs.at[d]
    node_wait(cb, cbr, K_C)
    zbs[...] = unpack(cbr[...])
    local_send(pick_zb, zbr, K_ZB)

    for p in range(NP):
        local_wait(pick_za[p], zar.at[p], K_ZA + p)
        gin_o[:, p * PW:(p + 1) * PW] = jnp.sum(zar[p].astype(F32), axis=0).astype(BF)
    local_wait(pick_zg, zgr, K_ZG)
    gg_o[...] = jnp.sum(zgr[...].astype(F32), axis=0).T[:TOP, :].astype(BF)
    local_wait(pick_zb, zbr, K_ZB)
    for c in range(NL):
        gin_o[:, DA + c * W:DA + (c + 1) * W] = zbr[c]

    local_done(tgm, K_META)
    node_done(gms, gmr, K_GM)
    node_done(gs, gr, K_G)
    node_done(cb, cbr, K_C)
    local_done(zgr, K_ZG)
    local_done(zbr, K_ZB)
    for t in range(2):
        local_done(tgb.at[t], K_TB + t)
        for h in range(2):
            node_done(sb.at[t, h], rb.at[t, l, h], K_B + 2 * t + h)
        for p in range(NP):
            node_done(sa.at[t, p], ra.at[t, p], K_A + t * NP + p)
        for s in range(4):
            for d in range(2):
                if s < 3 or d == t:
                    tok_ring(t, s, d).wait_send()
                for h in range(2):
                    if s < 3 or h == d:
                        ring(t, s, d, h).wait_send()
    for p in range(NP):
        node_done(pa.at[p], backa.at[p], K_PA + p)
        local_done(zar.at[p], K_ZA + p)
    for s in range(4):
        for d in range(2):
            for h in range(2):
                if s > 0 or h == d:
                    reduce_copy(s, d, h).wait_send()


def per_device(tokens, grad_out, expert_ids, gate_weights, w_gate, w_up, w_down):
    vm = pl.BlockSpec(memory_space=pltpu.VMEM)
    anywhere = pl.BlockSpec(memory_space=pl.ANY)
    shape = jax.ShapeDtypeStruct
    dma = pltpu.SemaphoreType.DMA
    gin, gg, gwg, gwu, gwd = pl.pallas_call(
        kernel,
        out_shape=(
            shape((TOK, D), BF), shape((TOP, TOK), BF),
            pltpu.VMEM((D, HB), BF), pltpu.VMEM((D, HB), BF), pltpu.VMEM((HB, D), BF),
        ),
        in_specs=[vm, vm, vm, vm, anywhere, anywhere, anywhere],
        out_specs=(vm, vm, vm, vm, vm),
        scratch_shapes=[
            pltpu.VMEM((D, 2 * HB), BF),
            pltpu.VMEM((HB, D), BF),
            pltpu.VMEM((8, 128), F32),
            pltpu.VMEM((8, 128), F32),
            pltpu.VMEM((NL, 8, 128), F32),
            pltpu.VMEM((2, NL, TOK, W), BF),
            pltpu.VMEM((2, NL, TOK, DA), BF),
            pltpu.VMEM((ROWS, NL * TOK), BF),
            pltpu.VMEM((NL * TOK, ROWS), BF),
            pltpu.VMEM((ROWS, 128), BF),
            pltpu.VMEM((ROWS, 128), BF),
            pltpu.VMEM((2, 2, ROWS, WH), BF),
            pltpu.VMEM((2, NL, 2, ROWS, WH), BF),
            pltpu.VMEM((2, NP, ROWS, PW), BF),
            pltpu.VMEM((2, NP, ROWS, PW), BF),
            pltpu.VMEM((ROWS, 2 * HB), F32),
            pltpu.VMEM((ROWS, HB), F32),
            pltpu.VMEM((ROWS, 2 * HB), BF),
            pltpu.VMEM((HB, ROWS), BF),
            pltpu.VMEM((NP, ROWS, PW), BF),
            pltpu.VMEM((NP, ROWS, PW), BF),
            pltpu.VMEM((ROWS, 128), BF),
            pltpu.VMEM((ROWS, 128), BF),
            pltpu.VMEM((4, 2, 2, HALF, W), BF),
            pltpu.VMEM((4, 2, 2, HALF, W), BF),
            pltpu.VMEM((ROWS, W), BF),
            pltpu.VMEM((ROWS, W), BF),
            pltpu.VMEM((NP, NL, TOK, PW), BF),
            pltpu.VMEM((NP, NL, TOK, PW), BF),
            pltpu.VMEM((NL, TOK, W), BF),
            pltpu.VMEM((NL, TOK, W), BF),
            pltpu.VMEM((NL, TOK, 128), BF),
            pltpu.VMEM((NL, TOK, 128), BF),
            dma((K_ALL,)), dma((K_ALL,)), dma((K_ALL,)),
            dma((2, 4, 2, 2)), dma((2, 4, 2, 2)), dma((4, 2, 2)), dma((4, 2, 2)),
            dma((2, 4, 2)), dma((2, 4, 2)), dma((3,)),
        ],
        compiler_params=pltpu.CompilerParams(
            collective_id=0, has_side_effects=True, vmem_limit_bytes=54 * 2**20
        ),
        name="expert_backward",
    )(tokens, grad_out, expert_ids.T, gate_weights.T, w_gate[0], w_up[0], w_down[0])
    return gin, gg.T, gwg[None], gwu[None], gwd[None]


def solution(mesh):
    rows = P(("node", "local"), None)
    columns = P("node", None, "local")
    return jax.shard_map(
        per_device,
        mesh=mesh,
        in_specs=(rows, rows, rows, rows, columns, columns, P("node", "local", None)),
        out_specs=(rows, rows, columns, columns, P("node", "local", None)),
        check_vma=False,
    )
```
